32 devices in a mesh: dp: 8 (over z, x), row: 2 (over y), col: 2 (over core).
Axes of the slice: x: 2, y: 2, z: 4, core: 2. Of those that a mesh axis runs over, the one named last changes fastest.
Arguments:
- inputs: float32 [6272, 512], P(('dp', 'col'), 'row'), may hold values from -6 to 6
- cotangent: float32 [6272, 512], P(('dp', 'col'), 'row'), may hold values from -6 to 6
- image_live: int32 [32], P(('dp', 'col')), may hold values 0 or 1
- region_ids: int32 [4, 49], replicated, may hold values from 0 to 2
- rel_index: int32 [49, 49], replicated, may hold values from 0 to 168
- norm1_gain: float32 [512], P('row'), may hold values from 0.5 to 1.5
- norm1_bias: float32 [512], P('row'), may hold values from -3 to 3
- qkv_weight: bfloat16 [512, 3, 512], P('row', None, 'col'), may hold values from -0.25 to 0.25
- qv_bias: float32 [2, 512], P(None, 'col'), may hold values from -3 to 3
- rel_table: float32 [169, 16], P(None, 'col'), may hold values from -3 to 245
- proj_weight: bfloat16 [512, 512], P('col', 'row'), may hold values from -1 to 1
- proj_bias: float32 [512], P('row'), may hold values from -3 to 3
- norm2_gain: float32 [512], P('row'), may hold values from 0.5 to 1.5
- norm2_bias: float32 [512], P('row'), may hold values from -3 to 3
- fc1_weight: bfloat16 [512, 2048], P('row', 'col'), may hold values from -0.25 to 0.25
- fc1_bias: float32 [2048], P('col'), may hold values from -3 to 3
- fc2_weight: bfloat16 [2048, 512], P('col', 'row'), may hold values from -0.125 to 0.125
- fc2_bias: float32 [512], P('row'), may hold values from -3 to 3
Outputs:
- outputs: float32 [6272, 512], P(('dp', 'col'), 'row')
- input_grad: float32 [6272, 512], P(('dp', 'col'), 'row')
- qkv_weight_grad: float32 [512, 3, 512], P('row', None, 'col')
- qv_bias_grad: float32 [2, 512], P(None, 'col')
- rel_table_grad: float32 [169, 16], replicated
- proj_weight_grad: float32 [512, 512], P('col', 'row')
- proj_bias_grad: float32 [512], P('row')
- fc1_weight_grad: float32 [512, 2048], P('row', 'col')
- fc1_bias_grad: float32 [2048], P('col')
- fc2_weight_grad: float32 [2048, 512], P('col', 'row')
- fc2_bias_grad: float32 [512], P('row')
- norm1_gain_grad: float32 [512], replicated
- norm1_bias_grad: float32 [512], replicated
- norm2_gain_grad: float32 [512], replicated
- norm2_bias_grad: float32 [512], replicated
The draws below stay inside these ranges and needn't reach their ends.
All inputs are finite; a program needn't handle non-finite values. No bound on the sum of `image_live` on one device may be relied on, other than what follows from the above.
Results may differ from the reference program's by a relative error of at most 0.0095.
Values may be sent and summed in bfloat16 or wider, within the bound.
No kernel may reach another device: no remote copies, remote signals or barrier semaphores. Data moves between devices by JAX's collectives and lax.ppermute only.
A program may use at most 64 MiB of HBM per device.

```python
import math
import jax
import jax.numpy as jnp
from jax import lax

D = 512
HEADS = 16
HEAD_DIM = 32
FF = 2048
SIDE = 14
WIN = 7
SHIFT = 3
IMG_TOK = 196
WIN_TOK = 49
WINDOWS = 4
TABLE = 169
IMAGES = 32
TOKENS = 6272


def draw_rel_table(key, part):
    base = jnp.clip(jax.random.normal(key, (TABLE, HEADS), jnp.float32), -3.0, 3.0)
    return base


def touch_ends(values, stream_key, least, top_value):
    longest = values.shape.index(max(values.shape))
    spots = []
    for shift in (0, 1):
        where = [jax.random.randint(jax.random.fold_in(stream_key, axis), (), 0, length) for axis, length in enumerate(values.shape)]
        where[longest] = (where[longest] + shift) % values.shape[longest]
        spots.append(tuple(where))
    return values.at[spots[0]].set(least).at[spots[1]].set(top_value)


def shard_levels(rng, dims, cuts, least, high):
    def one(dim, shards_of):
        steps = jax.random.uniform(jax.random.fold_in(jax.random.fold_in(rng, 6), dim), (shards_of,), jnp.float32, least / len(cuts), high / len(cuts))
        return jnp.repeat(jnp.exp(steps), dims[dim] // shards_of).reshape((-1,) + (1,) * (len(dims) - dim - 1))

    loudness = one(*cuts[0])
    for cut in cuts[1:]:
        loudness = loudness * one(*cut)
    return loudness


def normal_values(stream_key, extent, width, bound, cuts=(), dtype=jnp.bfloat16):
    result = width * jax.random.normal(stream_key, extent, jnp.float32)
    if cuts:
        result = result * shard_levels(stream_key, extent, cuts, -0.22, 0.18)
    return jnp.clip(result, -bound, bound).astype(dtype)


def setup_inputs(seed: int = 0) -> dict:
    key_of = jax.random.split(jax.random.key(seed), 19)
    return {
        "inputs": normal_values(key_of[0], (TOKENS, D), 1.0, 6.0, ((0, 16), (1, 2)), jnp.float32),
        "cotangent": normal_values(key_of[1], (TOKENS, D), 1.0, 6.0, ((0, 16), (1, 2)), jnp.float32),
        "image_live": touch_ends((jax.random.randint(key_of[2], (IMAGES,), 0, 4) < 3).astype(jnp.int32), jax.random.fold_in(key_of[2], 1), 0, 1),
        "region_ids": touch_ends(jax.random.randint(key_of[3], (WINDOWS, WIN_TOK), 0, 3), jax.random.fold_in(key_of[3], 1), 0, 2).astype(jnp.int32),
        "rel_index": touch_ends(jax.random.randint(key_of[4], (WIN_TOK, WIN_TOK), 0, TABLE), jax.random.fold_in(key_of[4], 1), 0, TABLE - 1).astype(jnp.int32),
        "norm1_gain": jnp.clip(1.0 + 0.1 * jax.random.normal(key_of[5], (D,), jnp.float32), 0.5, 1.5),
        "norm1_bias": normal_values(key_of[6], (D,), 0.3, 3.0, ((0, 2),), jnp.float32),
        "qkv_weight": normal_values(key_of[7], (D, 3, D), D ** -0.5, 0.25, ((0, 2), (2, 2))),
        "qv_bias": normal_values(key_of[8], (2, D), 0.5, 3.0, ((1, 2),), jnp.float32),
        "rel_table": draw_rel_table(jax.random.fold_in(key_of[18], 71), 0),
        "proj_weight": normal_values(key_of[10], (D, D), (D // 16) ** -0.5, 1.0, ((0, 2), (1, 2))),
        "proj_bias": normal_values(key_of[11], (D,), 0.5, 3.0, ((0, 2),), jnp.float32),
        "norm2_gain": jnp.clip(1.0 + 0.1 * jax.random.normal(key_of[12], (D,), jnp.float32), 0.5, 1.5),
        "norm2_bias": normal_values(key_of[13], (D,), 0.3, 3.0, ((0, 2),), jnp.float32),
        "fc1_weight": normal_values(key_of[14], (D, FF), D ** -0.5, 0.25, ((0, 2), (1, 2))),
        "fc1_bias": normal_values(key_of[15], (FF,), 0.5, 3.0, ((0, 2),), jnp.float32),
        "fc2_weight": normal_values(key_of[16], (FF, D), FF ** -0.5, 0.125, ((0, 2), (1, 2))),
        "fc2_bias": normal_values(key_of[17], (D,), 0.5, 3.0, ((0, 2),), jnp.float32),
    }


def to_windows(tokens):
    image_count = tokens.shape[0] // (SIDE * SIDE)
    trailing = tokens.shape[1:]
    tiling = tokens.reshape((image_count, SIDE, SIDE, -1))
    tiling = jnp.roll(tiling, (-SHIFT, -SHIFT), axis=(1, 2))
    across = SIDE // WIN
    tiling = tiling.reshape((image_count, across, WIN, across, WIN, tiling.shape[-1]))
    tiling = tiling.transpose((0, 1, 3, 2, 4, 5))
    return tiling.reshape((image_count, across * across, WIN * WIN) + trailing)

def from_windows(windows):
    image_count = windows.shape[0]
    trailing = windows.shape[3:]
    across = SIDE // WIN
    tiling = windows.reshape((image_count, across, across, WIN, WIN, -1)).transpose((0, 1, 3, 2, 4, 5))
    tiling = tiling.reshape((image_count, SIDE, SIDE, -1))
    tiling = jnp.roll(tiling, (SHIFT, SHIFT), axis=(1, 2))
    return tiling.reshape((image_count * SIDE * SIDE,) + trailing)

def norm_stats(rows):
    mean_val = lax.optimization_barrier(jnp.mean(rows, -1, keepdims=True))
    mean_sq = lax.optimization_barrier(jnp.mean(rows * rows, -1, keepdims=True))
    norm_scale = lax.rsqrt(mean_sq - mean_val * mean_val + 1e-05)
    return ((rows - mean_val) * norm_scale, norm_scale)

def norm_backward(dnorm, centered, norm_scale, gain):
    scaled = dnorm * gain
    first = lax.optimization_barrier(jnp.mean(scaled, -1, keepdims=True))
    second = lax.optimization_barrier(jnp.mean(scaled * centered, -1, keepdims=True))
    return norm_scale * (scaled - first - centered * second)

def cumulative(values):
    return 0.5 * (1.0 + jax.scipy.special.erf(values / math.sqrt(2.0)))

def gelu_slope(values):
    return cumulative(values) + values * jnp.exp(-0.5 * values * values) / math.sqrt(2.0 * math.pi)

def window_scores(windows, rel_bias, allowed):
    query = windows[:, :, :, 0].astype(jnp.float32)
    keys = windows[:, :, :, 1].astype(jnp.float32)
    scores = jnp.einsum('awihd,awjhd->awhij', query, keys) * HEAD_DIM ** (-0.5) + rel_bias
    return jnp.where(allowed[None, :, None], scores, -1e+30)

def attend_forward(windows, rel_bias, allowed):
    scores = window_scores(windows, rel_bias, allowed)
    highest = lax.optimization_barrier(jnp.max(scores, -1, keepdims=True))
    log_total = highest + jnp.log(lax.optimization_barrier(jnp.sum(jnp.exp(scores - highest), -1, keepdims=True)))
    probs = jnp.exp(scores - log_total).astype(jnp.bfloat16)
    values = windows[:, :, :, 2].astype(jnp.float32)
    attended = jnp.einsum('awhij,awjhd->awihd', probs.astype(jnp.float32), values)
    return (attended.astype(jnp.bfloat16), log_total)

def attend_backward(windows, rel_bias, allowed, log_total, dheads):
    scores = window_scores(windows, rel_bias, allowed)
    weights = jnp.exp(scores - log_total)
    rounded = weights.astype(jnp.bfloat16).astype(jnp.float32)
    query = windows[:, :, :, 0].astype(jnp.float32)
    keys = windows[:, :, :, 1].astype(jnp.float32)
    values = windows[:, :, :, 2].astype(jnp.float32)
    dheads_f = dheads.astype(jnp.float32)
    dvalues = jnp.einsum('awhij,awihd->awjhd', rounded, dheads_f)
    dweights = jnp.einsum('awihd,awjhd->awhij', dheads_f, values)
    dscores = weights * (dweights - lax.optimization_barrier(jnp.sum(dweights * weights, -1, keepdims=True)))
    dscores_b = dscores.astype(jnp.bfloat16).astype(jnp.float32)
    dquery = jnp.einsum('awhij,awjhd->awihd', dscores_b, keys) * HEAD_DIM ** (-0.5)
    dkeys = jnp.einsum('awhij,awihd->awjhd', dscores_b, query) * HEAD_DIM ** (-0.5)
    dwindows = jnp.stack([dquery, dkeys, dvalues], axis=3).astype(jnp.bfloat16)
    return (dwindows, lax.optimization_barrier(jnp.sum(dscores, axis=(0, 1))))

def reference(inputs, cotangent, image_live, region_ids, rel_index, norm1_gain, norm1_bias, qkv_weight, qv_bias, rel_table, proj_weight, proj_bias, norm2_gain, norm2_bias, fc1_weight, fc1_bias, fc2_weight, fc2_bias):
    block_images = math.gcd(IMAGES, 16)
    block_count = IMAGES // block_images
    rel_bias = rel_table[rel_index].transpose(2, 0, 1)
    allowed = region_ids[:, :, None] == region_ids[:, None, :]
    bias_rows = jnp.stack([qv_bias[0], jnp.zeros_like(qv_bias[0]), qv_bias[1]])
    flat_qkv = qkv_weight.reshape(D, 3 * D)

    def one_block(totals, pieces):
        rows_in, cot_in, live_in = pieces
        token_rows = rows_in.shape[0]
        centered1, scale1 = norm_stats(rows_in)
        normed1 = (centered1 * norm1_gain + norm1_bias).astype(jnp.bfloat16)
        qkv_rows = jnp.dot(normed1, flat_qkv, preferred_element_type=jnp.float32).reshape(token_rows, 3, D)
        qkv_rows = (qkv_rows + bias_rows).astype(jnp.bfloat16)
        windows = to_windows(qkv_rows.reshape(token_rows, 3, HEADS, HEAD_DIM))
        attended, log_total = attend_forward(windows, rel_bias, allowed)
        heads_rows = from_windows(attended).reshape(token_rows, D)
        middle = rows_in + (jnp.dot(heads_rows, proj_weight, preferred_element_type=jnp.float32) + proj_bias)
        centered2, scale2 = norm_stats(middle)
        normed2 = (centered2 * norm2_gain + norm2_bias).astype(jnp.bfloat16)
        pre_act = jnp.dot(normed2, fc1_weight, preferred_element_type=jnp.float32) + fc1_bias
        hidden = (pre_act * cumulative(pre_act)).astype(jnp.bfloat16)
        outputs = middle + (jnp.dot(hidden, fc2_weight, preferred_element_type=jnp.float32) + fc2_bias)
        live_cot = cot_in * jnp.repeat(live_in, IMG_TOK).astype(jnp.float32)[:, None]
        dmlp = live_cot.astype(jnp.bfloat16)
        fc2_grad = jnp.dot(hidden.T, dmlp, preferred_element_type=jnp.float32)
        fc2_bias_grad = lax.optimization_barrier(jnp.sum(dmlp.astype(jnp.float32), 0))
        dpre = (jnp.dot(dmlp, fc2_weight.T, preferred_element_type=jnp.float32) * gelu_slope(pre_act)).astype(jnp.bfloat16)
        fc1_grad = jnp.dot(normed2.T, dpre, preferred_element_type=jnp.float32)
        fc1_bias_grad = lax.optimization_barrier(jnp.sum(dpre.astype(jnp.float32), 0))
        dnorm2 = jnp.dot(dpre, fc1_weight.T, preferred_element_type=jnp.float32)
        dmiddle = live_cot + norm_backward(dnorm2, centered2, scale2, norm2_gain)
        gain2_grad = lax.optimization_barrier(jnp.sum(dnorm2 * centered2, 0))
        beta2_grad = lax.optimization_barrier(jnp.sum(dnorm2, 0))
        dattn = dmiddle.astype(jnp.bfloat16)
        proj_grad = jnp.dot(heads_rows.T, dattn, preferred_element_type=jnp.float32)
        proj_bias_grad = lax.optimization_barrier(jnp.sum(dattn.astype(jnp.float32), 0))
        dheads = jnp.dot(dattn, proj_weight.T, preferred_element_type=jnp.float32).astype(jnp.bfloat16)
        dwindows, dscore_sum = attend_backward(windows, rel_bias, allowed, log_total, to_windows(dheads.reshape(token_rows, HEADS, HEAD_DIM)))
        dqkv = from_windows(dwindows).reshape(token_rows, 3 * D)
        qkv_grad = jnp.dot(normed1.T, dqkv, preferred_element_type=jnp.float32).reshape(D, 3, D)
        qkv_sums = lax.optimization_barrier(jnp.sum(dqkv.astype(jnp.float32), 0)).reshape(3, D)
        qv_grad = jnp.stack([qkv_sums[0], qkv_sums[2]])
        dnorm1 = jnp.dot(dqkv, flat_qkv.T, preferred_element_type=jnp.float32)
        input_grad = dmiddle + norm_backward(dnorm1, centered1, scale1, norm1_gain)
        gain1_grad = lax.optimization_barrier(jnp.sum(dnorm1 * centered1, 0))
        beta1_grad = lax.optimization_barrier(jnp.sum(dnorm1, 0))
        table_grad = jnp.zeros((TABLE, HEADS), jnp.float32).at[rel_index.reshape(-1)].add(dscore_sum.transpose(1, 2, 0).reshape(-1, HEADS))
        fresh = (qkv_grad, qv_grad, table_grad, proj_grad, proj_bias_grad, fc1_grad, fc1_bias_grad, fc2_grad, fc2_bias_grad, gain1_grad, beta1_grad, gain2_grad, beta2_grad)
        return (jax.tree.map(jnp.add, totals, fresh), (outputs, input_grad))
    start = (jnp.zeros((D, 3, D), jnp.float32), jnp.zeros((2, D), jnp.float32), jnp.zeros((TABLE, HEADS), jnp.float32), jnp.zeros((D, D), jnp.float32), jnp.zeros((D,), jnp.float32), jnp.zeros((D, FF), jnp.float32), jnp.zeros((FF,), jnp.float32), jnp.zeros((FF, D), jnp.float32), jnp.zeros((D,), jnp.float32), jnp.zeros((D,), jnp.float32), jnp.zeros((D,), jnp.float32), jnp.zeros((D,), jnp.float32), jnp.zeros((D,), jnp.float32))
    totals, stacked = lax.scan(one_block, start, (inputs.reshape(block_count, -1, D), cotangent.reshape(block_count, -1, D), image_live.reshape(block_count, block_images)))
    outputs = stacked[0].reshape(TOKENS, D)
    input_grad = stacked[1].reshape(TOKENS, D)
    return (outputs, input_grad, totals[0], totals[1], totals[2], totals[3], totals[4], totals[5], totals[6], totals[7], totals[8], totals[9], totals[10], totals[11], totals[12])
```

```python
import math

import jax
import jax.numpy as jnp
import numpy as np
from jax import lax
from jax.experimental import pallas as pl
from jax.experimental.pallas import tpu as pltpu
from jax.sharding import PartitionSpec as P

HEAD_DIM = 32
SIDE = 14
WIN = 7
SHIFT = 3
IMG_TOK = SIDE * SIDE
WIN_TOK = WIN * WIN
ACROSS = SIDE // WIN
WINDOWS = ACROSS * ACROSS
SLOT = 64
ROWS = WINDOWS * SLOT
LANES = 128
GROUP = LANES // HEAD_DIM
BF = jnp.bfloat16
F32 = jnp.float32
NEG = -1e30


def window_matrix():
    perm = np.zeros((ROWS, IMG_TOK), np.float32)
    for a in range(SIDE):
        for b in range(SIDE):
            ra, rb = (a - SHIFT) % SIDE, (b - SHIFT) % SIDE
            row = ((ra // WIN) * ACROSS + rb // WIN) * SLOT + (ra % WIN) * WIN + rb % WIN
            perm[row, a * SIDE + b] = 1.0
    return perm


def mm(left, right):
    return lax.dot_general(left, right, (((1,), (0,)), ((), ())), preferred_element_type=F32)


def mm_rt(left, right):
    return lax.dot_general(left, right, (((1,), (1,)), ((), ())), preferred_element_type=F32)


def mm_lt(left, right):
    return lax.dot_general(left, right, (((0,), (0,)), ((), ())), preferred_element_type=F32)


def move_rows(matrix, values):
    high = values.astype(BF)
    low = (values - high.astype(F32)).astype(BF)
    return mm(matrix, high) + mm(matrix, low)


def call(kernel, outs, *args):
    return pl.pallas_call(
        kernel,
        out_shape=[jax.ShapeDtypeStruct(shape, dtype) for shape, dtype in outs],
        name=kernel.__name__,
    )(*args)


def stats(own, peer):
    width = own.shape[1] + peer.shape[1]
    mean = (jnp.sum(own, -1, keepdims=True) + jnp.sum(peer, -1, keepdims=True)) / width
    square = (
        jnp.sum(own * own, -1, keepdims=True) + jnp.sum(peer * peer, -1, keepdims=True)
    ) / width
    scale = lax.rsqrt(square - mean * mean + 1e-05)
    return (own - mean) * scale, (peer - mean) * scale, scale


def norm_back(dnorm, centered, scale, gains):
    width = sum(part.shape[1] for part in dnorm)
    scaled = [part * gain for part, gain in zip(dnorm, gains)]
    first = sum(jnp.sum(part, -1, keepdims=True) for part in scaled) / width
    second = (
        sum(jnp.sum(part * cent, -1, keepdims=True) for part, cent in zip(scaled, centered)) / width
    )
    return [scale * (part - first - cent * second) for part, cent in zip(scaled, centered)]


def block_diag(tile):
    row = lax.broadcasted_iota(jnp.int32, (GROUP * SLOT, LANES), 0) // SLOT
    lane = lax.broadcasted_iota(jnp.int32, (GROUP * SLOT, LANES), 1) // HEAD_DIM
    return jnp.where(row == lane, jnp.concatenate([tile] * GROUP, axis=0), jnp.zeros((), BF))


def take_heads(stacked):
    lane = lax.broadcasted_iota(jnp.int32, (SLOT, LANES), 1) // HEAD_DIM
    out = stacked[:SLOT]
    for head in range(1, GROUP):
        out = jnp.where(lane == head, stacked[head * SLOT : (head + 1) * SLOT], out)
    return out


def attention_forward(
    own_ref, recv_ref, ovec_ref, perm_ref, w00, w10, w01, w11, qb_ref, bias_ref, mask_ref,
    x_ref, n1_ref, q_ref, k_ref, v_ref, p_ref, heads_ref,
):
    half = own_ref.shape[1]
    perm = perm_ref[...]
    own = move_rows(perm, own_ref[...])
    peer = move_rows(perm, recv_ref[0:IMG_TOK, :])
    x_ref[:, :half] = own
    x_ref[:, half:] = peer
    cent_own, cent_peer, _ = stats(own, peer)
    pvec = recv_ref[IMG_TOK:, :]
    n_own = (cent_own * ovec_ref[0:1, :] + ovec_ref[1:2, :]).astype(BF)
    n_peer = (cent_peer * pvec[0:1, :] + pvec[1:2, :]).astype(BF)
    n1_ref[:, :half] = n_own
    n1_ref[:, half:] = n_peer
    for part, dest in enumerate((q_ref, k_ref, v_ref)):
        for col, (w_own, w_peer) in enumerate(((w00, w10), (w01, w11))):
            width = w_own.shape[2]
            total = mm(n_own, w_own[part]) + mm(n_peer, w_peer[part])
            if part != 1:
                total = total + qb_ref[part // 2 + 2 * col : part // 2 + 2 * col + 1, :]
            dest[:, col * width : (col + 1) * width] = total.astype(BF)

    groups = q_ref.shape[1] // LANES

    def one_window(win, carry):
        base = pl.multiple_of(win * SLOT, SLOT)
        allowed = mask_ref[win] > 0.0
        for grp in range(groups):
            lanes = slice(grp * LANES, (grp + 1) * LANES)
            query = block_diag(q_ref[pl.ds(base, SLOT), lanes])
            scores = mm_rt(k_ref[pl.ds(base, SLOT), lanes], query)
            scores = scores * HEAD_DIM ** (-0.5) + bias_ref[grp]
            scores = jnp.where(allowed, scores, NEG)
            top = jnp.max(scores, 0, keepdims=True)
            expo = jnp.exp(scores - top)
            weights = expo / jnp.sum(expo, 0, keepdims=True)
            spot = pl.multiple_of(win * (groups * SLOT) + grp * SLOT, SLOT)
            p_ref[pl.ds(spot, SLOT), :] = weights
            out = take_heads(mm_lt(weights.astype(BF), v_ref[pl.ds(base, SLOT), lanes]))
            heads_ref[pl.ds(base, SLOT), lanes] = out.astype(BF)
        return carry

    lax.fori_loop(0, WINDOWS, one_window, 0)


def feed_forward(
    x_ref, heads_ref, p00, p01, p10, p11, ovec_ref, pvec_ref, f00, f10, f01, f11, fb_ref,
    mid_ref, n2_ref, hid_ref, slope_ref,
):
    half = p00.shape[1]
    h_own = heads_ref[:, : p00.shape[0]]
    h_peer = heads_ref[:, p00.shape[0] :]
    m_own = x_ref[:, :half] + (mm(h_own, p00[...]) + mm(h_peer, p10[...]) + ovec_ref[4:5, :])
    m_peer = x_ref[:, half:] + (mm(h_own, p01[...]) + mm(h_peer, p11[...]) + pvec_ref[4:5, :])
    mid_ref[:, :half] = m_own
    mid_ref[:, half:] = m_peer
    cent_own, cent_peer, _ = stats(m_own, m_peer)
    n_own = (cent_own * ovec_ref[2:3, :] + ovec_ref[3:4, :]).astype(BF)
    n_peer = (cent_peer * pvec_ref[2:3, :] + pvec_ref[3:4, :]).astype(BF)
    n2_ref[:, :half] = n_own
    n2_ref[:, half:] = n_peer
    step = 256
    for col, (w_own, w_peer) in enumerate(((f00, f10), (f01, f11))):
        width = w_own.shape[1]
        for at in range(0, width, step):
            pre = mm(n_own, w_own[:, at : at + step]) + mm(n_peer, w_peer[:, at : at + step])
            pre = pre + fb_ref[col : col + 1, at : at + step]
            phi = 0.5 * (1.0 + lax.erf(pre * (1.0 / math.sqrt(2.0))))
            spot = slice(col * width + at, col * width + at + step)
            hid_ref[:, spot] = (pre * phi).astype(BF)
            slope = phi + pre * jnp.exp(-0.5 * pre * pre) * (1.0 / math.sqrt(2.0 * math.pi))
            slope_ref[:, spot] = slope.astype(BF)


def cotangent_windows(own_ref, recv_ref, perm_ref, cot_ref):
    half = own_ref.shape[1]
    cot_ref[:, :half] = move_rows(perm_ref[...], own_ref[...])
    cot_ref[:, half:] = move_rows(perm_ref[...], recv_ref[...])


def second_weight_grad(hid_ref, cot_ref, send_ref, keep_ref):
    half = cot_ref.shape[1] // 2
    width = hid_ref.shape[1] // 2
    for row in range(2):
        dm = cot_ref[:, row * half : (row + 1) * half].astype(BF)
        keep_ref[row] = mm_lt(hid_ref[:, :width], dm).astype(BF)
        send_ref[row] = mm_lt(hid_ref[:, width:], dm).astype(BF)


def second_layer(
    hid_ref, slope_ref, mid_ref, cot_ref, perm_ref, w00, w01, w10, w11, ovec_ref, pvec_ref,
    out_own_ref, out_peer_ref, dpre_ref,
):
    half = w00.shape[1]
    width = w00.shape[0]
    h_own = hid_ref[:, :width]
    h_peer = hid_ref[:, width:]
    back = perm_ref[...].T
    o_own = mid_ref[:, :half] + (mm(h_own, w00[...]) + mm(h_peer, w10[...]) + ovec_ref[5:6, :])
    o_peer = mid_ref[:, half:] + (mm(h_own, w01[...]) + mm(h_peer, w11[...]) + pvec_ref[5:6, :])
    out_own_ref[...] = move_rows(back, o_own)
    out_peer_ref[...] = move_rows(back, o_peer)
    d_own = cot_ref[:, :half].astype(BF)
    d_peer = cot_ref[:, half:].astype(BF)
    for col, (w_own, w_peer) in enumerate(((w00, w01), (w10, w11))):
        spot = slice(col * width, (col + 1) * width)
        dhid = mm_rt(d_own, w_own[...]) + mm_rt(d_peer, w_peer[...])
        dpre_ref[:, spot] = (dhid * slope_ref[:, spot].astype(F32)).astype(BF)


def first_weight_grad(n2_ref, dpre_ref, send_ref, keep_ref):
    half = n2_ref.shape[1] // 2
    width = dpre_ref.shape[1] // 2
    for row in range(2):
        norm = n2_ref[:, row * half : (row + 1) * half]
        keep_ref[row] = mm_lt(norm, dpre_ref[:, :width]).astype(BF)
        send_ref[row] = mm_lt(norm, dpre_ref[:, width:]).astype(BF)


def middle_backward(
    dpre_ref, f00, f10, f01, f11, mid_ref, cot_ref, ovec_ref, pvec_ref, heads_ref,
    p00, p01, p10, p11,
    dmid_ref, dheads_ref, gsend_ref, gkeep_ref, sums_ref, fsum_ref,
):
    half = f00.shape[0]
    width = f00.shape[1]
    dpre_own = dpre_ref[:, :width]
    dpre_peer = dpre_ref[:, width:]
    fsum_ref[:, :width] = jnp.sum(dpre_own.astype(F32), 0, keepdims=True)
    fsum_ref[:, width:] = jnp.sum(dpre_peer.astype(F32), 0, keepdims=True)
    dn = [
        mm_rt(dpre_own, f00[...]) + mm_rt(dpre_peer, f01[...]),
        mm_rt(dpre_own, f10[...]) + mm_rt(dpre_peer, f11[...]),
    ]
    cent_own, cent_peer, scale = stats(mid_ref[:, :half], mid_ref[:, half:])
    cent = [cent_own, cent_peer]
    parts = norm_back(dn, cent, scale, [ovec_ref[2:3, :], pvec_ref[2:3, :]])
    datt = []
    for row in range(2):
        spot = slice(row * half, (row + 1) * half)
        cot = cot_ref[:, spot]
        dmid = cot + parts[row]
        dmid_ref[:, spot] = dmid
        datt.append(dmid.astype(BF))
        sums_ref[0:1, spot] = jnp.sum(dn[row] * cent[row], 0, keepdims=True)
        sums_ref[1:2, spot] = jnp.sum(dn[row], 0, keepdims=True)
        sums_ref[2:3, spot] = jnp.sum(datt[row].astype(F32), 0, keepdims=True)
        sums_ref[3:4, spot] = jnp.sum(cot.astype(BF).astype(F32), 0, keepdims=True)
    part = p00.shape[0]
    for row in range(2):
        gkeep_ref[row] = mm_lt(heads_ref[:, :part], datt[row]).astype(BF)
        gsend_ref[row] = mm_lt(heads_ref[:, part:], datt[row]).astype(BF)
    for col, (w_own, w_peer) in enumerate(((p00, p01), (p10, p11))):
        dh = mm_rt(datt[0], w_own[...]) + mm_rt(datt[1], w_peer[...])
        dheads_ref[:, col * part : (col + 1) * part] = dh.astype(BF)


def attention_backward(
    q_ref, k_ref, v_ref, p_ref, dheads_ref, n1_ref,
    dqkv_ref, table_ref, gsend_ref, gkeep_ref, qsum_ref,
):
    groups = q_ref.shape[1] // LANES
    table_ref[...] = jnp.zeros_like(table_ref)
    factor = HEAD_DIM ** (-0.5)

    def one_window(win, carry):
        base = pl.multiple_of(win * SLOT, SLOT)
        rows = pl.ds(base, SLOT)
        for grp in range(groups):
            lanes = slice(grp * LANES, (grp + 1) * LANES)
            dout = block_diag(dheads_ref[rows, lanes])
            spot = pl.multiple_of(win * (groups * SLOT) + grp * SLOT, SLOT)
            weights = p_ref[pl.ds(spot, SLOT), :]
            dweights = mm_rt(v_ref[rows, lanes], dout)
            inner = jnp.sum(dweights * weights, 0, keepdims=True)
            dscores = weights * (dweights - inner)
            table_ref[grp] += dscores
            rounded = dscores.astype(BF)
            keys = k_ref[rows, lanes]
            query = block_diag(q_ref[rows, lanes])
            dqkv_ref[0, rows, lanes] = (take_heads(mm_lt(rounded, keys)) * factor).astype(BF)
            dqkv_ref[1, rows, lanes] = (mm(rounded, query) * factor).astype(BF)
            dqkv_ref[2, rows, lanes] = mm(weights.astype(BF), dout).astype(BF)
        return carry

    lax.fori_loop(0, WINDOWS, one_window, 0)
    half = n1_ref.shape[1] // 2
    width = q_ref.shape[1] // 2
    qsum_ref[...] = jnp.zeros_like(qsum_ref)
    for part in range(3):
        values = dqkv_ref[part]
        qsum_ref[part : part + 1, :] = jnp.sum(values.astype(F32), 0, keepdims=True)
        for row in range(2):
            norm = n1_ref[:, row * half : (row + 1) * half]
            gkeep_ref[row, part] = mm_lt(norm, values[:, :width]).astype(BF)
            gsend_ref[row, part] = mm_lt(norm, values[:, width:]).astype(BF)


def input_backward(
    dqkv_ref, w00, w10, w01, w11, x_ref, dmid_ref, ovec_ref, pvec_ref, perm_ref,
    own_ref, peer_ref, sums_ref,
):
    half = own_ref.shape[1]
    width = w00.shape[2]
    dn = []
    for w_own, w_peer in ((w00, w01), (w10, w11)):
        total = jnp.zeros((ROWS, half), F32)
        for part in range(3):
            total = total + mm_rt(dqkv_ref[part, :, :width], w_own[part])
            total = total + mm_rt(dqkv_ref[part, :, width:], w_peer[part])
        dn.append(total)
    cent_own, cent_peer, scale = stats(x_ref[:, :half], x_ref[:, half:])
    cent = [cent_own, cent_peer]
    parts = norm_back(dn, cent, scale, [ovec_ref[0:1, :], pvec_ref[0:1, :]])
    back = perm_ref[...].T
    own_ref[...] = move_rows(back, dmid_ref[:, :half] + parts[0])
    peer_ref[...] = move_rows(back, dmid_ref[:, half:] + parts[1])
    for row in range(2):
        spot = slice(row * half, (row + 1) * half)
        sums_ref[0:1, spot] = jnp.sum(dn[row] * cent[row], 0, keepdims=True)
        sums_ref[1:2, spot] = jnp.sum(dn[row], 0, keepdims=True)


def flip(values, axis, size, bit=1):
    return lax.ppermute(values, axis, [(i, i ^ bit) for i in range(size)])


def by_order(index, own, peer, axis=-1):
    return jnp.where(
        index == 0,
        jnp.concatenate([own, peer], axis),
        jnp.concatenate([peer, own], axis),
    )


def pick(index, both, axis=-1):
    size = both.shape[axis] // 2
    return lax.dynamic_slice_in_dim(both, index * size, size, both.ndim + axis if axis < 0 else axis)


def make_shards(dp_size):
    def dp_levels():
        bit = 1
        levels = []
        while bit < dp_size:
            levels.append(bit)
            bit *= 2
        return levels

    def dp_sum(part):
        place = lax.axis_index("dp")
        levels = dp_levels()
        for bit in levels:
            side = (place // bit) % 2
            size = part.shape[0] // 2
            send = lax.dynamic_slice_in_dim(part, (1 - side) * size, size, 0)
            kept = lax.dynamic_slice_in_dim(part, side * size, size, 0)
            got = flip(send, "dp", dp_size, bit)
            part = (kept.astype(F32) + got.astype(F32)).astype(BF)
        for bit in reversed(levels):
            side = (place // bit) % 2
            got = flip(part, "dp", dp_size, bit)
            part = by_order(side, part, got, 0)
        return part

    def grad_sum(send, keep, shape):
        got = flip(send, "col", 2)
        both = keep.astype(F32) + got.astype(F32)
        out = flip(both[1].astype(BF), "row", 2)
        part = (both[0] + out.astype(F32)).astype(BF)
        part = part.reshape(shape)
        return dp_sum(part)

    def shards(
        inputs, cotangent, image_live, region_ids, rel_index, norm1_gain, norm1_bias, qkv_weight,
        qv_bias, rel_table, proj_weight, proj_bias, norm2_gain, norm2_bias, fc1_weight, fc1_bias,
        fc2_weight, fc2_bias,
    ):
        row = lax.axis_index("row")
        col = lax.axis_index("col")
        half = inputs.shape[1]
        table_size, local_heads = rel_table.shape
        wide = fc1_weight.shape[1]
        perm = jnp.asarray(window_matrix(), BF)

        live = image_live.astype(F32)
        pack = jnp.stack([norm1_gain, norm1_bias, norm2_gain, norm2_bias, proj_bias, fc2_bias])
        ovec = jnp.pad(pack, ((0, 2), (0, 0)))
        other = lax.dynamic_slice_in_dim(inputs, (1 - row) * IMG_TOK, IMG_TOK, 0)
        own = lax.dynamic_slice_in_dim(inputs, row * IMG_TOK, IMG_TOK, 0)
        recv = flip(jnp.concatenate([other, ovec, jnp.zeros((4, half), F32)], 0), "row", 2)
        pvec = recv[IMG_TOK : IMG_TOK + 8]

        def spread(weight):
            down = flip(weight, "row", 2)
            return weight, down, flip(weight, "col", 2), flip(down, "col", 2)

        qw00, qw10, qw01, qw11 = spread(qkv_weight.transpose(1, 0, 2))
        colvec = jnp.concatenate([qv_bias, fc1_bias.reshape(-1, qv_bias.shape[1])], 0)
        colpeer = flip(colvec, "col", 2)
        table = jnp.concatenate([rel_table, flip(rel_table, "col", 2)], 1)
        qb = jnp.concatenate([qv_bias, colpeer[:2], jnp.zeros((4, qv_bias.shape[1]), F32)], 0)
        fb = jnp.stack([fc1_bias, colpeer[2:].reshape(-1)])

        pad = SLOT - WIN_TOK
        index = jnp.pad(rel_index.T, ((0, pad), (0, pad)), constant_values=-1)
        onehot = (index[:, :, None] == jnp.arange(table_size)[None, None, :]).astype(F32)
        heads = table.shape[1]
        groups = heads // GROUP
        bias = jnp.einsum("jit,th->hji", onehot, table, precision=lax.Precision.HIGHEST)
        bias = bias.reshape(groups, GROUP, SLOT, SLOT).transpose(0, 2, 1, 3)
        bias = bias.reshape(groups, SLOT, GROUP * SLOT)
        region = jnp.pad(region_ids, ((0, 0), (0, pad)), constant_values=-1)
        allowed = region[:, :, None] == region[:, None, :]
        real = jnp.arange(SLOT) < WIN_TOK
        allowed = (allowed | ~real[None, None, :]) & real[None, :, None]
        mask = jnp.tile(allowed.astype(F32), (1, 1, GROUP))

        cot_live = cotangent * jnp.repeat(live, IMG_TOK)[:, None]
        cot_other = lax.dynamic_slice_in_dim(cot_live, (1 - row) * IMG_TOK, IMG_TOK, 0)
        cot_own = lax.dynamic_slice_in_dim(cot_live, row * IMG_TOK, IMG_TOK, 0)

        width = 2 * half
        sq = (ROWS, heads * HEAD_DIM)
        x, n1, q, k, v, p, hd = call(
            attention_forward,
            [((ROWS, width), F32), ((ROWS, width), BF), (sq, BF), (sq, BF), (sq, BF),
             ((WINDOWS * groups * SLOT, GROUP * SLOT), F32), (sq, BF)],
            own, recv, ovec, perm, qw00, qw10, qw01, qw11, qb, bias, mask,
        )
        pw00, pw01, pw10, pw11 = spread(proj_weight)
        pw01, pw10 = pw01, pw10
        pj00, pj01, pj10, pj11 = pw00, pw01, pw10, pw11
        f00, f10, f01, f11 = spread(fc1_weight)
        mid, n2, hid, slope = call(
            feed_forward,
            [((ROWS, width), F32), ((ROWS, width), BF), ((ROWS, 2 * wide), BF),
             ((ROWS, 2 * wide), BF)],
            x, hd, pj00, pj01, pj10, pj11, ovec, pvec, f00, f10, f01, f11, fb,
        )
        cot_recv = flip(cot_other, "row", 2)
        (cot,) = call(cotangent_windows, [((ROWS, width), F32)], cot_own, cot_recv, perm)
        s00, s01, s10, s11 = spread(fc2_weight)
        grad_shape = ((2, wide, half), BF)
        send2, keep2 = call(second_weight_grad, [grad_shape, grad_shape], hid, cot)
        out_own, out_peer, dpre = call(
            second_layer,
            [((IMG_TOK, half), F32), ((IMG_TOK, half), F32), ((ROWS, 2 * wide), BF)],
            hid, slope, mid, cot, perm, s00, s01, s10, s11, ovec, pvec,
        )
        fc2_grad = grad_sum(send2, keep2, (wide, half))
        grad_shape = ((2, half, wide), BF)
        send1, keep1 = call(first_weight_grad, [grad_shape, grad_shape], n2, dpre)
        fc1_grad = grad_sum(send1, keep1, (half, wide))
        part = qv_bias.shape[1]
        dmid, dheads, psend, pkeep, sums2, fsum = call(
            middle_backward,
            [((ROWS, width), F32), (sq, BF), ((2, part, half), BF), ((2, part, half), BF),
             ((8, width), F32), ((1, 2 * wide), F32)],
            dpre, f00, f10, f01, f11, mid, cot, ovec, pvec, hd, pj00, pj01, pj10, pj11,
        )
        dqkv, tsum, qsend, qkeep, qsum = call(
            attention_backward,
            [((3,) + sq, BF), ((groups, SLOT, GROUP * SLOT), F32), ((2, 3, half, part), BF),
             ((2, 3, half, part), BF), ((8, 2 * part), F32)],
            q, k, v, p, dheads, n1,
        )
        last_send = jnp.concatenate([psend[:, None], qsend], 1)
        last_keep = jnp.concatenate([pkeep[:, None], qkeep], 1)
        last = grad_sum(last_send, last_keep, (4 * half, part)).reshape(4, half, part)
        in_own, in_peer, sums1 = call(
            input_backward,
            [((IMG_TOK, half), F32), ((IMG_TOK, half), F32), ((8, width), F32)],
            dqkv, qw00, qw10, qw01, qw11, x, dmid, ovec, pvec, perm,
        )

        out_recv = flip(out_peer, "row", 2)
        outputs = by_order(row, out_own, out_recv, 0)
        in_recv = flip(in_peer, "row", 2)
        input_grad = by_order(row, in_own, in_recv, 0)

        tsum = tsum.reshape(groups, SLOT, GROUP, SLOT)
        table_part = jnp.einsum(
            "gjhi,jit->ght", tsum, onehot, precision=lax.Precision.HIGHEST
        ).reshape(heads, table_size)
        table_part = by_order(col, table_part[:local_heads], table_part[local_heads:], 0)
        by_row = jnp.concatenate([sums1[:2], sums2[:4]], 0)
        by_row = by_order(row, by_row[:, :half], by_row[:, half:])
        fsum = by_order(col, fsum[0, :wide], fsum[0, wide:])
        qsum = by_order(col, qsum[:, :part], qsum[:, part:])
        flat = jnp.concatenate(
            [by_row.reshape(-1), fsum, qsum[0], qsum[2], table_part.reshape(-1)]
        )
        total = flat.shape[0]
        flat = jnp.pad(flat, (0, -total % 1024)).reshape(-1, LANES)
        flat = flat + flip(flat, "col", 2)
        flat = flat + flip(flat, "row", 2)
        for bit in dp_levels():
            flat = flat + flip(flat, "dp", dp_size, bit)
        flat = flat.reshape(-1)
        rows6 = flat[: 6 * width].reshape(6, width)
        at = 6 * width
        fc1_bias_grad = pick(col, flat[at : at + 2 * wide], 0)
        at += 2 * wide
        qv_grad = pick(col, flat[at : at + 4 * part].reshape(2, 2 * part))
        at += 4 * part
        table_grad = flat[at : at + heads * table_size].reshape(heads, table_size).T
        return (
            outputs,
            input_grad,
            last[1:].astype(F32).transpose(1, 0, 2),
            qv_grad,
            table_grad,
            last[0].astype(F32),
            pick(row, rows6[4], 0),
            fc1_grad.astype(F32),
            fc1_bias_grad,
            fc2_grad.astype(F32),
            pick(row, rows6[5], 0),
            rows6[0],
            rows6[1],
            rows6[2],
            rows6[3],
        )

    return shards


def solution(mesh):
    tokens = P(("dp", "col"), "row")
    return jax.shard_map(
        make_shards(mesh.shape["dp"]),
        mesh=mesh,
        in_specs=(
            tokens, tokens, P(("dp", "col")), P(), P(), P("row"), P("row"),
            P("row", None, "col"), P(None, "col"), P(None, "col"), P("col", "row"), P("row"),
            P("row"), P("row"), P("row", "col"), P("col"), P("col", "row"), P("row"),
        ),
        out_specs=(
            tokens, tokens, P("row", None, "col"), P(None, "col"), P(), P("col", "row"),
            P("row"), P("row", "col"), P("col"), P("col", "row"), P("row"), P(), P(), P(), P(),
        ),
        check_vma=False,
    )
```
